32 devices in a mesh: samp: 8 (over y, x, core), cls: 4 (over z).
Axes of the slice: x: 2, y: 2, z: 4, core: 2. Of those that a mesh axis runs over, the one named last changes fastest.
Arguments:
- samples: bfloat16 [1024, 32768], P('samp'), may hold values from -0.046875 to 0.046875
- labels: int32 [1024], P('samp'), may hold values from 0 to 511
- weight: bfloat16 [32768, 512], P('samp', 'cls'), may hold values from -6 to 6
- dual: float32 [1024, 512], P('samp', 'cls'), may hold values from 0 to 1
- block_inverse: float32 [64, 16, 16], P('samp'), may hold values from -0.4 to 1.2, as said below
Outputs:
- new_weight: float32 [32768, 512], P('samp', 'cls')
- new_dual: float32 [1024, 512], P('samp', 'cls')
- class_gap: float32 [512], P('cls')
- top_margin: float32 [1024], P('samp')
The draws below stay inside these ranges and needn't reach their ends.
Inputs may be any that keep to these rules, and one draw needn't show every extreme that they name: `block_inverse`: each [16, 16] matrix has a positive diagonal.
All inputs are finite; a program needn't handle non-finite values.
Results may differ from the reference program's by a relative error of at most 0.00045.
Values may be sent and summed in bfloat16 or wider, within the bound.
A program may use at most 128 MiB of HBM per device.

```python
import jax
import jax.numpy as jnp
from jax import lax

FEATURES = 32768
CLASSES = 512
ROWS_DEV = 128
BLOCK = 16
PASSES = 2
SAMPLES = 1024
N_SAMP = 8


def draw_block_inverse(key, part):
    first, second = jax.random.split(jax.random.fold_in(key, 11))
    shape = (SAMPLES // BLOCK, BLOCK, BLOCK)
    spread = jnp.clip(jax.random.normal(second, shape, jnp.float32) * 0.08, -0.4, 0.4)
    diagonal = jax.random.uniform(first, (SAMPLES // BLOCK, BLOCK), jnp.float32, 0.6, 1.2)
    identity = jnp.eye(BLOCK, dtype=jnp.float32)
    return spread * (1.0 - identity) + diagonal[:, :, None] * identity


def with_ends(entries, rng, least, largest):
    index_at = [jax.random.randint(jax.random.fold_in(rng, axis), (), 0, length) for axis, length in enumerate(entries.shape)]
    widest = entries.shape.index(max(entries.shape))
    beside = index_at[:widest] + [(index_at[widest] + 1) % entries.shape[widest]] + index_at[widest + 1:]
    return entries.at[tuple(index_at)].set(least).at[tuple(beside)].set(largest)


def raised(entries, stream_key, source, target, blocks, factor):
    owner, partner = [(jnp.arange(entries.shape[axis_at]) // (entries.shape[axis_at] // blocks)).reshape([-1 if axis == axis_at else 1 for axis in range(entries.ndim)]) for axis_at in (source, target)]
    chosen = jax.random.permutation(stream_key, blocks)[partner]
    strong = (owner == chosen) | (owner == (partner + blocks // 2) % blocks)
    return jnp.where(strong, factor * entries, entries)


def block_scale(rng, shape, pieces, least, largest):
    def one(dim, parts):
        draws = jax.random.uniform(jax.random.fold_in(jax.random.fold_in(rng, 6), dim), (parts,), jnp.float32, least / len(pieces), largest / len(pieces))
        return jnp.repeat(jnp.exp(draws), shape[dim] // parts).reshape((-1,) + (1,) * (len(shape) - dim - 1))

    level = one(*pieces[0])
    for cut in pieces[1:]:
        level = level * one(*cut)
    return level


def noise(own_key, shape, scale, bound, cuts=(), held_as=jnp.bfloat16):
    gain = block_scale(own_key, shape, cuts, -0.22, 0.18) if cuts else 1.0
    result = jax.random.normal(own_key, shape, jnp.float32) * scale * gain
    return jnp.minimum(jnp.maximum(result, -bound), bound).astype(held_as)


def gaussian_with(stream_key, shape, width, reach, cuts, heavy, kind=jnp.bfloat16):
    values = width * jax.random.normal(stream_key, shape, jnp.float32)
    if cuts:
        values = values * block_scale(stream_key, shape, cuts, -0.22, 0.18)
    return jnp.clip(raised(values, jax.random.fold_in(stream_key, 3), *heavy), -reach, reach).astype(kind)


def setup_inputs(seed: int = 0) -> dict:
    key_of = jax.random.split(jax.random.key(seed), 6)
    samples = gaussian_with(key_of[0], (SAMPLES, FEATURES), (FEATURES ** -0.5), 0.046875, ((0, 8),), (0, 1, 8, 2.0))
    labels = with_ends(jax.random.randint(key_of[1], (SAMPLES,), 0, CLASSES), jax.random.fold_in(key_of[1], 1), 0, CLASSES - 1).astype(jnp.int32)
    weight = noise(key_of[2], (FEATURES, CLASSES), 1.0, 6.0, ((0, 8), (1, 4)))
    dual = jnp.clip(1.0 * jax.random.uniform(key_of[3], (SAMPLES, CLASSES), jnp.float32) ** block_scale(key_of[3], (SAMPLES, CLASSES), ((0, 8), (1, 4)), -0.2, 0.2), 0.0, 1.0)
    block_inverse = draw_block_inverse(jax.random.fold_in(key_of[5], 71), 0)
    return {"samples": samples, "labels": labels, "weight": weight, "dual": dual, "block_inverse": block_inverse}


coupling = 0.5


def dual_passes(gram, start, sign, dual, inverse):
    rows = start.shape[0]
    blocks = rows // BLOCK

    def visit(turn, carry):
        alpha, change = carry
        index = (turn % blocks).astype(jnp.int32)
        low = (index * BLOCK).astype(jnp.int32)
        gram_rows = lax.dynamic_slice_in_dim(gram, low, BLOCK, 0)
        start_rows = lax.dynamic_slice_in_dim(start, low, BLOCK, 0)
        sign_rows = lax.dynamic_slice_in_dim(sign, low, BLOCK, 0)
        dual_rows = lax.dynamic_slice_in_dim(dual, low, BLOCK, 0)
        alpha_rows = lax.dynamic_slice_in_dim(alpha, low, BLOCK, 0)
        matrix = lax.dynamic_index_in_dim(inverse, index, 0, keepdims=False)
        margin = start_rows + coupling * jnp.dot(gram_rows, change, precision=lax.Precision.HIGHEST)
        ascent = jnp.dot(matrix, 1.0 - sign_rows * margin, precision=lax.Precision.HIGHEST)
        alpha_rows = jnp.clip(alpha_rows + ascent, 0.0, 1.0)
        change_rows = sign_rows * (alpha_rows - dual_rows)
        alpha = lax.dynamic_update_slice_in_dim(alpha, alpha_rows, low, 0)
        change = lax.dynamic_update_slice_in_dim(change, change_rows, low, 0)
        return alpha, change

    alpha, change = lax.fori_loop(0, PASSES * blocks, visit, (dual, jnp.zeros_like(dual)))
    margin = start + coupling * jnp.dot(gram, change, precision=lax.Precision.HIGHEST)
    return alpha, margin, change


def reference(samples, labels, weight, dual, block_inverse):
    class_ids = jnp.arange(CLASSES, dtype=jnp.int32)
    sign = jnp.where(labels[:, None] == class_ids[None, :], 1.0, -1.0).astype(jnp.float32)
    start = jnp.dot(samples, weight, preferred_element_type=jnp.float32)
    scaled = sign * start
    terms = jnp.maximum(0.0, 1.0 - scaled) + dual * (scaled - 1.0)
    class_gap = jnp.sum(terms, axis=0) / SAMPLES

    blocks = ROWS_DEV // BLOCK

    def group(inputs):
        rows_x, rows_start, rows_sign, rows_dual, rows_inv = inputs
        gram = lax.dot_general(rows_x, rows_x, (((1,), (1,)), ((), ())), preferred_element_type=jnp.float32)
        return dual_passes(gram, rows_start, rows_sign, rows_dual, rows_inv)

    alpha, margin, change = lax.map(group, (
        samples.reshape(N_SAMP, ROWS_DEV, FEATURES),
        start.reshape(N_SAMP, ROWS_DEV, CLASSES),
        sign.reshape(N_SAMP, ROWS_DEV, CLASSES),
        dual.reshape(N_SAMP, ROWS_DEV, CLASSES),
        block_inverse.reshape(N_SAMP, blocks, BLOCK, BLOCK)))
    new_dual = alpha.reshape(SAMPLES, CLASSES)
    top_margin = jnp.max(margin.reshape(SAMPLES, CLASSES), axis=1)
    steps = change.reshape(SAMPLES, CLASSES).astype(jnp.bfloat16)
    delta = lax.dot_general(samples, steps, (((0,), (0,)), ((), ())), preferred_element_type=jnp.float32)
    new_weight = weight.astype(jnp.float32) + coupling * delta
    return new_weight, new_dual, class_gap, top_margin
```

```python
import functools

import jax
import jax.numpy as jnp
from jax import lax
from jax.experimental import pallas as pl
from jax.experimental.pallas import tpu as pltpu
from jax.sharding import PartitionSpec as P

PASSES = 2
coupling = 0.5
MESH = pl.DeviceIdType.MESH
SUBS = 2
F32 = jnp.float32


def flip(index, mask, n):
    out = 0
    bit = 1
    while bit < n:
        digit = (index // bit) % 2
        if mask & bit:
            digit = 1 - digit
        out = out + digit * bit
        bit *= 2
    return out


def shares(d, F, split):
    hops = bin(d >> 1).count("1")
    if not split or hops == 0:
        return 0
    if hops == 1:
        return max(F * 5 // 16 // 128 * 128, 128)
    return F // 2 // 128 * 128


def kernel(n, ncls, BLOCK, samples, labels_col, weight, dual, inverse,
           new_weight, new_dual, class_gap, top_margin,
           a_all, x_buf, w_buf, gb, ib, gram, margin, sign, dual_v, alpha, change, inv_v, lab_v,
           p_buf, r_buf, gap_out, gap_in, top_out, top_in, s_out, s_all, o_buf,
           send_split, recv_split, send_fwd, recv_fwd, send_direct, recv_direct,
           x_sem, in_sem, send_p, recv_p, send_g, recv_g, send_t, recv_t, send_s, recv_s, out_sem):
    s = lax.axis_index("samp")
    c = lax.axis_index("cls")
    rows, N = samples.shape
    F = N // n
    width = weight.shape[1]
    par = c % 2
    pair = c + 1 - 2 * par
    split = ncls % 2 == 0
    peer = {d: flip(s, d, n) for d in range(1, n)}
    step_rows = rows // SUBS

    barrier = pltpu.get_barrier_semaphore()
    for d in range(1, n):
        pl.semaphore_signal(barrier, inc=1, device_id=(peer[d], c), device_id_type=MESH)
    for j in range(1, ncls):
        pl.semaphore_signal(barrier, inc=1, device_id=(s, (c + j) % ncls), device_id_type=MESH)
    pl.semaphore_wait(barrier, n - 1 + ncls - 1)

    def remote(src, dst, ssem, rsem, dev):
        return pltpu.make_async_remote_copy(src_ref=src, dst_ref=dst, send_sem=ssem, recv_sem=rsem,
                                            device_id=dev, device_id_type=MESH)

    def cols(start, size):
        return pl.ds(pl.multiple_of(start, 128), size)

    one_hop = [d for d in range(1, n) if bin(d >> 1).count("1") == 1]
    far = [d for d in range(1, n) if bin(d >> 1).count("1") > 1]
    near = [d for d in range(1, n) if d >> 1 == 0]
    one_hop = [d for d in one_hop if d % 2 == 0] + [d for d in one_hop if d % 2]
    order = [(d, k) for d in one_hop for k in range(SUBS)]
    order = sorted(order, key=lambda e: (e[1], one_hop.index(e[0])))
    order = order + [(d, k) for d in far for k in range(SUBS)]
    order = [e for e in order if shares(e[0], F, split)]
    finals = []

    split_copy, fwd_copy, direct_copy = {}, {}, {}
    for d, k in order:
        h = shares(d, F, split)
        rs = pl.ds(k * step_rows, step_rows)
        copy = remote(samples.at[rs, cols(peer[d] * F + par * h, h)],
                      a_all.at[s, rs, cols(par * h, h)],
                      send_split.at[d, k], recv_split.at[d, k], (peer[d], c))
        copy.start()
        split_copy[d, k] = copy
    for d in near + one_hop + far:
        h = shares(d, F, split)
        if 2 * h < F:
            copy = remote(samples.at[:, cols(peer[d] * F + 2 * h, F - 2 * h)],
                          a_all.at[s, :, 2 * h:F],
                          send_direct.at[d], recv_direct.at[d], (peer[d], c))
            copy.start()
            direct_copy[d] = copy

    loads = []
    for i, (src, dst) in enumerate([(samples.at[:, cols(s * F, F)], a_all.at[s]), (weight, w_buf),
                                    (dual, dual_v), (inverse, inv_v), (labels_col, lab_v)]):
        load = pltpu.make_async_copy(src, dst, in_sem.at[i])
        load.start()
        loads.append(load)
    x_loads = []
    for i in range(n):
        load = pltpu.make_async_copy(samples.at[:, i * F:(i + 1) * F], x_buf.at[i], x_sem.at[i])
        load.start()
        x_loads.append(load)

    def gram_piece(i):
        x_loads[i].wait()
        x = x_buf[i]
        part = lax.dot_general(x, x, (((1,), (1,)), ((), ())), preferred_element_type=F32)
        gram[...] = part if i == 0 else gram[...] + part

    def broadcast_piece(i):
        g = coupling * gram[...]
        for k in range(i * BLOCK, (i + 1) * BLOCK):
            gb[k] = jnp.broadcast_to(g[:, k:k + 1], (rows, width))

    def inverse_piece():
        for k in range(BLOCK):
            ib[k] = jnp.broadcast_to(inv_v[:, k:k + 1], (rows, width))
        ids = c * width + lax.broadcasted_iota(jnp.int32, (rows, width), 1)
        sign[...] = jnp.where(lab_v[...] == ids, 1.0, -1.0).astype(F32)
        alpha[...] = dual_v[...]
        change[...] = jnp.zeros((rows, width), F32)

    def own_piece():
        p_buf[0] = jnp.dot(a_all[s], w_buf[...], preferred_element_type=F32)

    work = [functools.partial(gram_piece, i) for i in range(n)]
    work += [own_piece, inverse_piece]
    work += [functools.partial(broadcast_piece, i) for i in range(rows // BLOCK)]
    per = -(-len(work) // max(len(order), 1))

    partial_copy = {}

    def partial_of(d):
        if d in direct_copy:
            direct_copy[d].wait_recv()
        if shares(d, F, split):
            for k in range(SUBS):
                fwd_copy[d, k].wait_recv()
        p_buf[d] = jnp.dot(a_all[peer[d]], w_buf[...], preferred_element_type=F32)
        copy = remote(p_buf.at[d], r_buf.at[d], send_p.at[d], recv_p.at[d], (peer[d], c))
        copy.start()
        partial_copy[d] = copy

    for load in loads:
        load.wait()
    for d, k in order:
        h = shares(d, F, split)
        rs = pl.ds(k * step_rows, step_rows)
        split_copy[d, k].wait_recv()
        src = a_all.at[peer[d], rs, cols(par * h, h)]
        copy = remote(src, src, send_fwd.at[d, k], recv_fwd.at[d, k], (s, pair))
        copy.start()
        fwd_copy[d, k] = copy
        for _ in range(per):
            if work:
                work.pop(0)()
    while work:
        work.pop(0)()
    for d in near + one_hop + far:
        partial_of(d)

    start = p_buf[0]
    for d in range(1, n):
        partial_copy[d].wait_recv()
        start = start + r_buf[d]
    margin[...] = start
    scaled = sign[...] * start
    terms = jnp.maximum(0.0, 1.0 - scaled) + dual_v[...] * (scaled - 1.0)
    gap = jnp.sum(terms, axis=0, keepdims=True)
    gap_out[...] = jnp.broadcast_to(gap, gap_out.shape)
    gap_copy = []
    for d in range(1, n):
        copy = remote(gap_out, gap_in.at[d], send_g.at[d], recv_g.at[d], (peer[d], c))
        copy.start()
        gap_copy.append(copy)

    blocks = rows // BLOCK

    def visit(turn, carry):
        low = pl.multiple_of((turn % blocks) * BLOCK, BLOCK)
        here = pl.ds(low, BLOCK)
        sign_b = sign[here, :]
        residual = 1.0 - sign_b * margin[here, :]
        ascent = jnp.zeros((BLOCK, width), F32)
        for k in range(BLOCK):
            ascent = ascent + ib[k, here, :] * residual[k:k + 1, :]
        alpha_b = jnp.clip(alpha[here, :] + ascent, 0.0, 1.0)
        change_b = sign_b * (alpha_b - dual_v[here, :])
        moved = change_b - change[here, :]
        alpha[here, :] = alpha_b
        change[here, :] = change_b
        total = margin[...]
        for k in range(BLOCK):
            total = total + gb[low + k] * moved[k:k + 1, :]
        margin[...] = total
        return carry

    lax.fori_loop(0, PASSES * blocks, visit, 0)

    s_out[...] = change[...].astype(jnp.bfloat16)
    step_copy = []
    for d in far + one_hop + near:
        copy = remote(s_out, s_all.at[s], send_s.at[d], recv_s.at[d], (peer[d], c))
        copy.start()
        step_copy.append(copy)
    s_all[s] = s_out[...]
    top = jnp.max(margin[...].T, axis=0, keepdims=True)
    top_out[...] = jnp.broadcast_to(top, top_out.shape)
    top_copy = []
    for j in range(1, ncls):
        copy = remote(top_out, top_in.at[j], send_t.at[j], recv_t.at[j], (s, (c + j) % ncls))
        copy.start()
        top_copy.append(copy)
    dual_store = pltpu.make_async_copy(alpha, new_dual, out_sem.at[0])
    dual_store.start()
    for copy in step_copy:
        copy.wait_recv()
    steps = s_all[...].reshape(n * rows, width)
    chunks = o_buf.shape[0]
    tile = F // chunks
    stores = []
    for i in range(chunks):
        a = a_all[:, :, i * tile:(i + 1) * tile].reshape(n * rows, tile)
        delta = lax.dot_general(a, steps, (((0,), (0,)), ((), ())), preferred_element_type=F32)
        o_buf[i] = w_buf[i * tile:(i + 1) * tile, :].astype(F32) + coupling * delta
        store = pltpu.make_async_copy(o_buf.at[i], new_weight.at[i * tile:(i + 1) * tile, :], out_sem.at[1 + i])
        store.start()
        stores.append(store)

    gap_sum = gap
    for d, copy in zip(range(1, n), gap_copy):
        copy.wait_recv()
        gap_sum = gap_sum + gap_in[d, 0:1, :]
    class_gap[...] = gap_sum / (rows * n)
    best = top
    for j, copy in zip(range(1, ncls), top_copy):
        copy.wait_recv()
        best = jnp.maximum(best, top_in[j, 0:1, :])
    top_margin[...] = best

    for copy in (list(split_copy.values()) + list(fwd_copy.values()) + list(direct_copy.values())
                 + list(partial_copy.values()) + gap_copy + step_copy + top_copy):
        copy.wait_send()
    dual_store.wait()
    for store in stores:
        store.wait()


def fused(n, ncls, samples, labels, weight, dual, block_inverse):
    rows, N = samples.shape
    F, width = weight.shape
    block = block_inverse.shape[1]
    inverse = block_inverse.reshape(rows, block)
    any_spec = pl.BlockSpec(memory_space=pl.ANY)
    vmem = pl.BlockSpec(memory_space=pltpu.VMEM)
    chunks = max(F // 512, 1)
    square = pltpu.VMEM((rows, width), F32)
    dma = pltpu.SemaphoreType.DMA
    outs = pl.pallas_call(
        functools.partial(kernel, n, ncls, block),
        out_shape=(jax.ShapeDtypeStruct((F, width), F32), jax.ShapeDtypeStruct((rows, width), F32),
                   jax.ShapeDtypeStruct((1, width), F32), jax.ShapeDtypeStruct((1, rows), F32)),
        in_specs=[any_spec] * 5,
        out_specs=(any_spec, any_spec, vmem, vmem),
        scratch_shapes=[
            pltpu.VMEM((n, rows, F), jnp.bfloat16), pltpu.VMEM((n, rows, F), jnp.bfloat16),
            pltpu.VMEM((F, width), jnp.bfloat16),
            pltpu.VMEM((rows, rows, width), F32), pltpu.VMEM((block, rows, width), F32),
            pltpu.VMEM((rows, rows), F32), square, square, square, square, square,
            pltpu.VMEM((rows, block), F32), pltpu.VMEM((rows, 1), jnp.int32),
            pltpu.VMEM((n, rows, width), F32), pltpu.VMEM((n, rows, width), F32),
            pltpu.VMEM((8, width), F32), pltpu.VMEM((n, 8, width), F32),
            pltpu.VMEM((8, rows), F32), pltpu.VMEM((ncls, 8, rows), F32),
            pltpu.VMEM((rows, width), jnp.bfloat16), pltpu.VMEM((n, rows, width), jnp.bfloat16),
            pltpu.VMEM((chunks, F // chunks, width), F32),
            dma((n, SUBS)), dma((n, SUBS)), dma((n, SUBS)), dma((n, SUBS)), dma((n,)), dma((n,)),
            dma((n,)), dma((5,)), dma((n,)), dma((n,)), dma((n,)), dma((n,)), dma((ncls,)), dma((ncls,)),
            dma((n,)), dma((n,)), dma((1 + chunks,)),
        ],
        compiler_params=pltpu.CompilerParams(collective_id=0, has_side_effects=True,
                                             vmem_limit_bytes=60 * 2 ** 20),
    )(samples, labels[:, None], weight, dual, inverse)
    new_weight, new_dual, gap, top = outs
    return new_weight, new_dual, gap.reshape(-1), top.reshape(-1)


def solution(mesh):
    n, ncls = mesh.shape["samp"], mesh.shape["cls"]
    placed = (P("samp", None), P("samp"), P("samp", "cls"), P("samp", "cls"), P("samp", None, None))
    return jax.shard_map(
        functools.partial(fused, n, ncls),
        mesh=mesh,
        in_specs=placed,
        out_specs=(P("samp", "cls"), P("samp", "cls"), P("cls"), P("samp")),
        check_vma=False,
    )
```

```python
import functools

import jax
import jax.numpy as jnp
from jax import lax
from jax.experimental import pallas as pl
from jax.experimental.pallas import tpu as pltpu
from jax.sharding import PartitionSpec as P

PASSES = 2
coupling = 0.5
MESH = pl.DeviceIdType.MESH
SUBS = 2
ONE = 5
RING = False
F32 = jnp.float32


def flip(index, mask, n):
    out = 0
    bit = 1
    while bit < n:
        digit = (index // bit) % 2
        if mask & bit:
            digit = 1 - digit
        out = out + digit * bit
        bit *= 2
    return out


def shares(d, F, split):
    hops = bin(d >> 1).count("1")
    if not split or hops == 0:
        return 0
    if hops == 1:
        return max(F * ONE // 16 // 128 * 128, 128)
    return F // 2 // 128 * 128


def kernel(n, ncls, BLOCK, samples, labels_row, weight, dual, inverse,
           new_weight, new_dual, class_gap, top_margin,
           a_all, x_buf, w_buf, gb, ib, gram, margin, sign, dual_v, alpha, change, inv_v, lab_v,
           p_buf, r_buf, gap_out, gap_in, top_out, top_in, s_out, s_all, o_buf,
           send_split, recv_split, send_fwd, recv_fwd, send_direct, recv_direct,
           x_sem, in_sem, send_p, recv_p, send_g, recv_g, send_t, recv_t, send_s, recv_s, out_sem):
    s = lax.axis_index("samp")
    c = lax.axis_index("cls")
    rows, N = samples.shape
    F = N // n
    width = weight.shape[1]
    par = c % 2
    pair = [c + 1 - 2 * par, (c - 1 + 2 * par + ncls) % ncls]
    split = ncls % 2 == 0
    peer = {d: flip(s, d, n) for d in range(1, n)}
    step_rows = rows // SUBS

    barrier = pltpu.get_barrier_semaphore()
    for d in range(1, n):
        pl.semaphore_signal(barrier, inc=1, device_id=(peer[d], c), device_id_type=MESH)
    for j in range(1, ncls):
        pl.semaphore_signal(barrier, inc=1, device_id=(s, (c + j) % ncls), device_id_type=MESH)
    pl.semaphore_wait(barrier, n - 1 + ncls - 1)

    def remote(src, dst, ssem, rsem, dev):
        return pltpu.make_async_remote_copy(src_ref=src, dst_ref=dst, send_sem=ssem, recv_sem=rsem,
                                            device_id=dev, device_id_type=MESH)

    def cols(start, size):
        return pl.ds(pl.multiple_of(start, 128), size)

    one_hop = [d for d in range(1, n) if bin(d >> 1).count("1") == 1]
    far = [d for d in range(1, n) if bin(d >> 1).count("1") > 1]
    near = [d for d in range(1, n) if d >> 1 == 0]
    one_hop = [d for d in one_hop if d % 2 == 0] + [d for d in one_hop if d % 2]
    order = [(d, k) for d in one_hop for k in range(SUBS)]
    order = sorted(order, key=lambda e: (e[1], one_hop.index(e[0])))
    order = order + [(d, k) for d in far for k in range(SUBS)]
    order = [e for e in order if shares(e[0], F, split)]
    finals = []

    split_copy, fwd_copy, direct_copy = {}, {}, {}
    for d, k in order:
        h = shares(d, F, split)
        rs = pl.ds(k * step_rows, step_rows)
        copy = remote(samples.at[rs, cols(peer[d] * F + par * h, h)],
                      a_all.at[s, rs, cols(par * h, h)],
                      send_split.at[d, k], recv_split.at[d, k], (peer[d], c))
        copy.start()
        split_copy[d, k] = copy
    for d in near + one_hop + far:
        h = shares(d, F, split)
        if 2 * h < F:
            copy = remote(samples.at[:, cols(peer[d] * F + 2 * h, F - 2 * h)],
                          a_all.at[s, :, 2 * h:F],
                          send_direct.at[d], recv_direct.at[d], (peer[d], c))
            copy.start()
            direct_copy[d] = copy

    loads = []
    for i, (src, dst) in enumerate([(samples.at[:, cols(s * F, F)], a_all.at[s]), (weight, w_buf),
                                    (dual, dual_v), (inverse, inv_v), (labels_row, lab_v)]):
        load = pltpu.make_async_copy(src, dst, in_sem.at[i])
        load.start()
        loads.append(load)
    x_loads = []
    for i in range(n):
        load = pltpu.make_async_copy(samples.at[:, i * F:(i + 1) * F], x_buf.at[i], x_sem.at[i])
        load.start()
        x_loads.append(load)

    def gram_piece(i):
        x_loads[i].wait()
        x = x_buf[i]
        part = lax.dot_general(x, x, (((1,), (1,)), ((), ())), preferred_element_type=F32)
        gram[...] = part if i == 0 else gram[...] + part

    def broadcast_piece(i):
        g = coupling * gram[...]
        for k in range(i * BLOCK, (i + 1) * BLOCK):
            gb[k] = jnp.broadcast_to(g[:, k:k + 1], (rows, width))

    def inverse_piece():
        for k in range(BLOCK):
            ib[k] = jnp.broadcast_to(inv_v[:, k:k + 1], (rows, width))
        ids = c * width + lax.broadcasted_iota(jnp.int32, (rows, width), 1)
        sign[...] = jnp.where(jnp.broadcast_to(lab_v[...], (width, rows)).T == ids, 1.0, -1.0).astype(F32)
        alpha[...] = dual_v[...]
        change[...] = jnp.zeros((rows, width), F32)

    def own_piece():
        p_buf[0] = jnp.dot(a_all[s], w_buf[...], preferred_element_type=F32)

    work = [functools.partial(gram_piece, i) for i in range(n)]
    work += [own_piece, inverse_piece]
    work += [functools.partial(broadcast_piece, i) for i in range(rows // BLOCK)]
    per = -(-len(work) // max(len(order), 1))

    partial_copy = {}

    def product(d, low, size):
        here = cols(low, size)
        return jnp.dot(a_all[peer[d], :, here], w_buf[here, :], preferred_element_type=F32)

    def early(d):
        h = shares(d, F, split)
        if 2 * h == F:
            p_buf[d] = product(d, par * h, h)
        elif h:
            for k in range(SUBS):
                fwd_copy[d, k].wait_recv()
            p_buf[d] = product(d, 0, 2 * h)

    def late(d):
        h = shares(d, F, split)
        if 2 * h == F:
            for k in range(SUBS):
                fwd_copy[d, k].wait_recv()
            p_buf[d] = p_buf[d] + product(d, (1 - par) * h, h)
        else:
            direct_copy[d].wait_recv()
            rest = product(d, 2 * h, F - 2 * h)
            p_buf[d] = p_buf[d] + rest if h else rest
        copy = remote(p_buf.at[d], r_buf.at[d], send_p.at[d], recv_p.at[d], (peer[d], c))
        copy.start()
        partial_copy[d] = copy

    for load in loads:
        load.wait()
    for d, k in order:
        h = shares(d, F, split)
        rs = pl.ds(k * step_rows, step_rows)
        split_copy[d, k].wait_recv()
        src = a_all.at[peer[d], rs, cols(par * h, h)]
        copy = remote(src, src, send_fwd.at[d, k], recv_fwd.at[d, k], (s, pair[k % 2 if RING else 0]))
        copy.start()
        fwd_copy[d, k] = copy
        for _ in range(per):
            if work:
                work.pop(0)()
    while work:
        work.pop(0)()
    for d in near:
        late(d)
    for d in far + one_hop:
        early(d)
    for d in far + one_hop:
        late(d)

    start = p_buf[0]
    for d in range(1, n):
        partial_copy[d].wait_recv()
        start = start + r_buf[d]
    margin[...] = start
    p_buf[0] = start

    blocks = rows // BLOCK

    def visit(turn, carry):
        low = pl.multiple_of((turn % blocks) * BLOCK, BLOCK)
        here = pl.ds(low, BLOCK)
        sign_b = sign[here, :]
        residual = 1.0 - sign_b * margin[here, :]
        ascent = jnp.zeros((BLOCK, width), F32)
        for k in range(BLOCK):
            ascent = ascent + ib[k, here, :] * residual[k:k + 1, :]
        alpha_b = jnp.clip(alpha[here, :] + ascent, 0.0, 1.0)
        change_b = sign_b * (alpha_b - dual_v[here, :])
        moved = change_b - change[here, :]
        alpha[here, :] = alpha_b
        change[here, :] = change_b
        total = margin[...]
        for k in range(BLOCK):
            total = total + gb[low + k] * moved[k:k + 1, :]
        margin[...] = total
        return carry

    lax.fori_loop(0, PASSES * blocks, visit, 0)

    s_out[...] = change[...].astype(jnp.bfloat16)
    step_copy = []
    for d in far + one_hop + near:
        copy = remote(s_out, s_all.at[s], send_s.at[d], recv_s.at[d], (peer[d], c))
        copy.start()
        step_copy.append(copy)
    s_all[s] = s_out[...]
    scaled = sign[...] * p_buf[0]
    terms = jnp.maximum(0.0, 1.0 - scaled) + dual_v[...] * (scaled - 1.0)
    gap = jnp.sum(terms, axis=0, keepdims=True)
    gap_out[...] = jnp.broadcast_to(gap, gap_out.shape)
    gap_copy = []
    for d in range(1, n):
        copy = remote(gap_out, gap_in.at[d], send_g.at[d], recv_g.at[d], (peer[d], c))
        copy.start()
        gap_copy.append(copy)
    top = jnp.max(margin[...].T, axis=0, keepdims=True)
    top_out[...] = jnp.broadcast_to(top, top_out.shape)
    top_copy = []
    for j in range(1, ncls):
        copy = remote(top_out, top_in.at[j], send_t.at[j], recv_t.at[j], (s, (c + j) % ncls))
        copy.start()
        top_copy.append(copy)
    dual_store = pltpu.make_async_copy(alpha, new_dual, out_sem.at[0])
    dual_store.start()
    for copy in step_copy:
        copy.wait_recv()
    steps = s_all[...].reshape(n * rows, width)
    chunks = o_buf.shape[0]
    tile = F // chunks
    stores = []
    for i in range(chunks):
        a = a_all[:, :, i * tile:(i + 1) * tile].reshape(n * rows, tile)
        delta = lax.dot_general(a, steps, (((0,), (0,)), ((), ())), preferred_element_type=F32)
        o_buf[i] = w_buf[i * tile:(i + 1) * tile, :].astype(F32) + coupling * delta
        store = pltpu.make_async_copy(o_buf.at[i], new_weight.at[i * tile:(i + 1) * tile, :], out_sem.at[1 + i])
        store.start()
        stores.append(store)

    gap_sum = gap
    for d, copy in zip(range(1, n), gap_copy):
        copy.wait_recv()
        gap_sum = gap_sum + gap_in[d, 0:1, :]
    class_gap[...] = gap_sum / (rows * n)
    best = top
    for j, copy in zip(range(1, ncls), top_copy):
        copy.wait_recv()
        best = jnp.maximum(best, top_in[j, 0:1, :])
    top_margin[...] = best

    for copy in (list(split_copy.values()) + list(fwd_copy.values()) + list(direct_copy.values())
                 + list(partial_copy.values()) + gap_copy + step_copy + top_copy):
        copy.wait_send()
    dual_store.wait()
    for store in stores:
        store.wait()


def fused(n, ncls, samples, labels, weight, dual, block_inverse):
    rows, N = samples.shape
    F, width = weight.shape
    block = block_inverse.shape[1]
    inverse = block_inverse.reshape(rows, block)
    any_spec = pl.BlockSpec(memory_space=pl.ANY)
    vmem = pl.BlockSpec(memory_space=pltpu.VMEM)
    chunks = max(F // 512, 1)
    square = pltpu.VMEM((rows, width), F32)
    dma = pltpu.SemaphoreType.DMA
    outs = pl.pallas_call(
        functools.partial(kernel, n, ncls, block),
        out_shape=(jax.ShapeDtypeStruct((F, width), F32), jax.ShapeDtypeStruct((rows, width), F32),
                   jax.ShapeDtypeStruct((1, width), F32), jax.ShapeDtypeStruct((1, rows), F32)),
        in_specs=[any_spec] * 5,
        out_specs=(any_spec, any_spec, vmem, vmem),
        scratch_shapes=[
            pltpu.VMEM((n, rows, F), jnp.bfloat16), pltpu.VMEM((n, rows, F), jnp.bfloat16),
            pltpu.VMEM((F, width), jnp.bfloat16),
            pltpu.VMEM((rows, rows, width), F32), pltpu.VMEM((block, rows, width), F32),
            pltpu.VMEM((rows, rows), F32), square, square, square, square, square,
            pltpu.VMEM((rows, block), F32), pltpu.VMEM((1, rows), jnp.int32),
            pltpu.VMEM((n, rows, width), F32), pltpu.VMEM((n, rows, width), F32),
            pltpu.VMEM((8, width), F32), pltpu.VMEM((n, 8, width), F32),
            pltpu.VMEM((8, rows), F32), pltpu.VMEM((ncls, 8, rows), F32),
            pltpu.VMEM((rows, width), jnp.bfloat16), pltpu.VMEM((n, rows, width), jnp.bfloat16),
            pltpu.VMEM((chunks, F // chunks, width), F32),
            dma((n, SUBS)), dma((n, SUBS)), dma((n, SUBS)), dma((n, SUBS)), dma((n,)), dma((n,)),
            dma((n,)), dma((5,)), dma((n,)), dma((n,)), dma((n,)), dma((n,)), dma((ncls,)), dma((ncls,)),
            dma((n,)), dma((n,)), dma((1 + chunks,)),
        ],
        compiler_params=pltpu.CompilerParams(collective_id=0, has_side_effects=True,
                                             vmem_limit_bytes=60 * 2 ** 20),
    )(samples, labels[None, :], weight, dual, inverse)
    new_weight, new_dual, gap, top = outs
    return new_weight, new_dual, gap.reshape(-1), top.reshape(-1)


def solution(mesh):
    n, ncls = mesh.shape["samp"], mesh.shape["cls"]
    placed = (P("samp", None), P("samp"), P("samp", "cls"), P("samp", "cls"), P("samp", None, None))
    return jax.shard_map(
        functools.partial(fused, n, ncls),
        mesh=mesh,
        in_specs=placed,
        out_specs=(P("samp", "cls"), P("samp", "cls"), P("cls"), P("samp")),
        check_vma=False,
    )
```
